512 devices in a mesh: dp: 8 (over y_hi, x), feat: 64 (over y_lo, z, core).
Axes of the slice: x: 4, y: 4 (y_hi: 2, y_lo: 2; y = y_hi * 2 + y_lo), z: 16, core: 2. Of those that a mesh axis runs over, the one named last changes fastest.
Arguments:
- residuals: bfloat16 [384, 2, 8192], P('feat', None, 'dp'), may hold values from -6 to 6
- enc_w: bfloat16 [2, 8192, 16384], P(None, 'dp', 'feat'), may hold values from -0.046875 to 0.046875
- enc_b: float32 [16384], P('feat'), may hold values from 0.5 to 3
- dec_w: bfloat16 [2, 16384, 8192], P(None, 'feat', 'dp'), may hold values from -0.75 to 0.75
- dec_b: float32 [2, 8192], P(None, 'dp'), may hold values from -3 to 3
- active: int32 [384, 64], replicated, may hold values from 0 to 16383, all different within a row
Outputs:
- recon: bfloat16 [384, 2, 8192], P('feat', None, 'dp')
- enc_grad: bfloat16 [2, 8192, 16384], P(None, 'dp', 'feat')
- enc_bias_grad: float32 [16384], P('feat')
- dec_grad: bfloat16 [2, 16384, 8192], P(None, 'feat', 'dp')
- dec_bias_grad: float32 [2, 8192], P(None, 'dp')
The draws below stay inside these ranges and needn't reach their ends.
Inputs may be any that keep to these rules, and one draw needn't show every extreme that they name: Each row of active names 64 different features, and every feature is named by some row.
All inputs are finite; a program needn't handle non-finite values.
Results may differ from the reference program's by a relative error of at most 0.0062.
Values may be sent and summed in bfloat16 or wider, within the bound.
A program may use at most 64 MiB of HBM per device.

```python
import jax
import jax.numpy as jnp
from jax import lax

D = 8192
F = 16384
L = 2
K = 64
TOKENS = 384


def level_of(key, dims, pieces, least, high):
    gain = 1.0
    for position, parts in pieces:
        steps = jax.random.uniform(jax.random.fold_in(jax.random.fold_in(key, 6), position), (parts,), jnp.float32, least / len(pieces), high / len(pieces))
        gain = gain * jnp.repeat(jnp.exp(steps), dims[position] // parts).reshape((-1,) + (1,) * (len(dims) - 1 - position))
    return gain


def picks_of(rng, rows, count, top, lift):
    ranking = jax.random.permutation(jax.random.fold_in(rng, 1), count)
    boost = ranking
    for power in range(3):
        boost = boost * boost // count
    boost = boost * lift // count
    chance = jax.random.randint(jax.random.fold_in(rng, 2), (rows, count), 0, 4096) + boost
    fixed_rows = jax.random.permutation(jax.random.fold_in(rng, 3), rows)[jnp.arange(count) % rows]
    chance = jnp.where(jnp.arange(rows)[:, None] == fixed_rows[None, :], 1 << 14, chance)
    score = chance * count + jnp.arange(count)
    return lax.top_k(score.astype(jnp.int32), top)[1].astype(jnp.int32)


def bell_draw(own_key, shape, width, most, split=(), kind=jnp.bfloat16):
    values = jax.random.normal(own_key, shape, jnp.float32) * width
    if len(split) > 0:
        values = level_of(own_key, shape, split, -0.22, 0.18) * values
    return jnp.clip(values, min=-most, max=most).astype(kind)


def setup_inputs(seed: int = 0) -> dict:
    arg_keys = jax.random.split(jax.random.key(seed), 7)
    residuals = bell_draw(arg_keys[0], (TOKENS, L, D), 1.0, 6.0, ((0, 64), (2, 8)))
    enc_w = bell_draw(arg_keys[1], (L, D, F), (L * D) ** -0.5, 0.046875, ((1, 8), (2, 64)))
    enc_b = jnp.clip(0.5 + 2.5 * jax.random.uniform(arg_keys[2], (F,), jnp.float32) ** level_of(arg_keys[2], (F,), ((0, 64),), -0.2, 0.2), 0.5, 3.0)
    dec_w = bell_draw(arg_keys[3], (L, F, D), K ** -0.5, 0.75, ((1, 64), (2, 8)))
    dec_b = bell_draw(arg_keys[4], (L, D), 0.5, 3.0, ((1, 8),), jnp.float32)
    active = picks_of(arg_keys[5], TOKENS, F, K, 0)
    return {"residuals": residuals, "enc_w": enc_w, "enc_b": enc_b, "dec_w": dec_w, "dec_b": dec_b, "active": active}


def reference(residuals, enc_w, enc_b, dec_w, dec_b, active):
    flat_in = residuals.reshape(TOKENS, L * D)
    pre_act = jnp.dot(flat_in, enc_w.reshape(L * D, F), preferred_element_type=jnp.float32) + enc_b.astype(jnp.float32)
    row_ids = jnp.arange(TOKENS, dtype=jnp.int32)[:, None]
    mask_table = jnp.zeros((TOKENS, F), jnp.float32).at[row_ids, active].set(1.0)
    activation = (jnp.maximum(pre_act, 0.0) * mask_table).astype(jnp.bfloat16)
    recon_full = jnp.stack([jnp.dot(activation, dec_w[layer_idx], preferred_element_type=jnp.float32) for layer_idx in range(L)], axis=1)
    recon_full = recon_full + dec_b.astype(jnp.float32)[None]
    recon = recon_full.astype(jnp.bfloat16)
    resid_grad = ((recon_full - residuals.astype(jnp.float32)) * 0.25).astype(jnp.bfloat16)
    dec_bias_grad = jnp.sum(resid_grad.astype(jnp.float32), axis=0)
    dec_grad = jnp.stack([jnp.dot(activation.T, resid_grad[:, layer_idx, :], preferred_element_type=jnp.float32) for layer_idx in range(L)], axis=0).astype(jnp.bfloat16)
    act_grad = jnp.dot(resid_grad[:, 0, :], dec_w[0].T, preferred_element_type=jnp.float32)
    for layer_idx in range(1, L):
        act_grad = act_grad + jnp.dot(resid_grad[:, layer_idx, :], dec_w[layer_idx].T, preferred_element_type=jnp.float32)
    pre_grad = jnp.where(activation > 0, act_grad, 0.0).astype(jnp.bfloat16)
    enc_bias_grad = jnp.sum(pre_grad.astype(jnp.float32), axis=0)
    enc_grad = jnp.dot(flat_in.T, pre_grad, preferred_element_type=jnp.float32).reshape(L, D, F).astype(jnp.bfloat16)
    return (recon, enc_grad, enc_bias_grad, dec_grad, dec_bias_grad)
```

```python
import functools

import jax
import jax.numpy as jnp
from jax import lax
from jax.experimental import pallas as pl
from jax.experimental.pallas import tpu as pltpu
from jax.sharding import PartitionSpec as P

MESH = pl.DeviceIdType.MESH
NZ = 16
F32 = jnp.float32
BF16 = jnp.bfloat16


def rdma(src, dst, send, recv, **where):
    return pltpu.make_async_remote_copy(
        src_ref=src, dst_ref=dst, send_sem=send, recv_sem=recv, device_id=where, device_id_type=MESH
    )


def place():
    me = lax.axis_index("feat")
    return me // 32, (me // 2) % NZ, me % 2


def feat_of(y, z, c):
    return (y * NZ + z) * 2 + c


def turn(i):
    odd = i % 2
    return (odd * ((i + 1) // 2) + (1 - odd) * (NZ - i // 2)) % NZ


def greet_feat():
    y, z, c = place()
    barrier = pltpu.get_barrier_semaphore()

    def signal(target):
        pl.semaphore_signal(barrier, inc=1, device_id={"feat": target}, device_id_type=MESH)

    def one(i, carry):
        signal(feat_of(y, (z + i) % NZ, c))
        return carry

    lax.fori_loop(1, NZ, one, 0)
    signal(feat_of(1 - y, z, c))
    signal(feat_of(y, z, 1 - c))
    signal(feat_of(1 - y, z, 1 - c))
    pl.semaphore_wait(barrier, NZ + 2)


def gather_feat(out, sems):
    zs, zr, ys, yr, cs, cr, ds, dr = sems
    y, z, c = place()
    half = out.shape[3] // 2

    def chunk(layer, zz, part):
        return out.at[layer, zz, :, pl.ds(pl.multiple_of(part * half, half), half)]

    def z_copy(s):
        return rdma(chunk(y, z, c), chunk(y, z, c), zs.at[s], zr.at[s], feat=feat_of(y, (z + s) % NZ, c))

    def z_arrival(s):
        piece = chunk(y, (z + NZ - s) % NZ, c)
        return rdma(piece, piece, zs.at[s], zr.at[s], feat=feat_of(y, (z + s) % NZ, c))

    def y_copy(s, layer):
        piece = chunk(layer, (z + NZ - s) % NZ, c)
        return rdma(piece, piece, ys.at[s], yr.at[s], feat=feat_of(1 - y, z, c))

    def c_copy(s, part):
        piece = chunk(y, (z + NZ - s) % NZ, part)
        return rdma(piece, piece, cs.at[s], cr.at[s], feat=feat_of(y, z, 1 - c))

    def d_copy(s, part):
        piece = chunk(1 - y, (z + NZ - s) % NZ, part)
        return rdma(piece, piece, ds.at[s], dr.at[s], feat=feat_of(y, z, 1 - c))

    def send(i, carry):
        z_copy(turn(NZ - i)).start()
        return carry

    def forward(i, carry):
        s = turn(i)

        @pl.when(i > 0)
        def _():
            z_arrival(s).wait_recv()

        y_copy(s, y).start()
        c_copy(s, c).start()

        @pl.when(i > 0)
        def _():
            before = turn(i - 1)
            y_copy(before, 1 - y).wait_recv()
            d_copy(before, c).start()

        return carry

    def finish(s, carry):
        @pl.when(s > 0)
        def _():
            z_copy(s).wait_send()

        y_copy(s, y).wait_send()
        c_copy(s, c).wait_send()
        d_copy(s, c).wait_send()
        c_copy(s, 1 - c).wait_recv()
        d_copy(s, 1 - c).wait_recv()
        return carry

    lax.fori_loop(1, NZ, send, 0)
    lax.fori_loop(0, NZ, forward, 0)
    last = turn(NZ - 1)
    y_copy(last, 1 - y).wait_recv()
    d_copy(last, c).start()
    lax.fori_loop(0, NZ, finish, 0)


GATHER_SEMS = [pltpu.SemaphoreType.DMA((NZ,))] * 8


def others(y, z, c):
    return (feat_of(1 - y, z, c), 1 - y, c), (feat_of(y, z, 1 - c), y, 1 - c), (feat_of(1 - y, z, 1 - c), 1 - y, 1 - c)


def gather_kernel(x_ref, out, got, gs, gr, *sems):
    y, z, c = place()
    half = x_ref.shape[2] // 2

    def cols(part):
        return pl.ds(pl.multiple_of(part * half, half), half)

    greet_feat()
    copies = [
        rdma(x_ref.at[yy, :, cols(cc)], got.at[k], gs.at[k], gr.at[k], feat=peer)
        for k, (peer, yy, cc) in enumerate(others(y, z, c))
    ]
    for copy in copies:
        copy.start()
    total = x_ref[y, :, cols(c)].astype(F32)
    for k, copy in enumerate(copies):
        copy.wait_recv()
        total = total + got[k].astype(F32)
    out[y, z, :, cols(c)] = total.astype(BF16)
    gather_feat(out, sems)
    for copy in copies:
        copy.wait_send()


def reduce_kernel(part, resid, bias, grad, recon, ra, rb, ry, rz, sy, sz, ss, sr, ws, wr, vs, vr, gs, gr, *sems):
    y, z, c = place()
    half = part.shape[3] // 2

    def cols(p):
        return pl.ds(pl.multiple_of(p * half, half), half)

    greet_feat()
    sibling = feat_of(y, z, 1 - c)
    first = rdma(part.at[1 - y, :, :, cols(1 - c)], ra, ss.at[0], sr.at[0], feat=sibling)
    second = rdma(part.at[y, :, :, cols(1 - c)], rb, ss.at[1], sr.at[1], feat=sibling)
    first.start()
    second.start()

    def y_copy(zz):
        return rdma(sy.at[zz], ry.at[zz], ws.at[zz], wr.at[zz], feat=feat_of(1 - y, z, c))

    def z_copy(s):
        return rdma(sz.at[s], rz.at[s], vs.at[s], vr.at[s], feat=feat_of(y, (z + s) % NZ, c))

    def to_y(i, carry):
        zz = (z + turn(NZ - 1 - i)) % NZ
        sy[zz] = (part[1 - y, zz, :, cols(c)] + ra[zz]).astype(BF16)
        y_copy(zz).start()
        return carry

    def to_z(i, carry):
        s = turn(NZ - 1 - i)
        zz = (z + s) % NZ
        y_copy(zz).wait_recv()
        sz[s] = (part[y, zz, :, cols(c)] + rb[zz] + ry[zz].astype(F32)).astype(BF16)
        z_copy(s).start()
        return carry

    first.wait_recv()
    lax.fori_loop(0, NZ, to_y, 0)
    second.wait_recv()
    lax.fori_loop(0, NZ - 1, to_z, 0)
    y_copy(z).wait_recv()
    total = part[y, z, :, cols(c)] + rb[z] + ry[z].astype(F32)

    def add(i, total):
        s = turn(i)
        z_copy(s).wait_recv()
        return total + rz[s].astype(F32)

    total = lax.fori_loop(1, NZ, add, total)
    full = total + bias[y, :, cols(c)]
    grad[y, z, :, cols(c)] = ((full - resid[y, z, :, cols(c)].astype(F32)) * 0.25).astype(BF16)
    recon[y, :, cols(c)] = full.astype(BF16)
    gather_feat(grad, sems)
    mine = recon.at[y, :, cols(c)]
    copies = [rdma(mine, mine, gs.at[k], gr.at[k], feat=peer) for k, (peer, _, _) in enumerate(others(y, z, c))]
    for copy in copies:
        copy.start()
    first.wait_send()
    second.wait_send()

    def drain(i, carry):
        y_copy(i).wait_send()

        @pl.when(i > 0)
        def _():
            z_copy(i).wait_send()

        return carry

    lax.fori_loop(0, NZ, drain, 0)
    for k, (peer, yy, cc) in enumerate(others(y, z, c)):
        copies[k].wait_send()
        piece = recon.at[yy, :, cols(cc)]
        rdma(piece, piece, gs.at[k], gr.at[k], feat=peer).wait_recv()


def dp_sum_kernel(finish, n, part, *refs):
    extra, (out, got, ps, pr, qs, qr) = refs[:-6], refs[-6:]
    me = lax.axis_index("dp")
    barrier = pltpu.get_barrier_semaphore()
    for s in range(1, n):
        pl.semaphore_signal(barrier, inc=1, device_id={"dp": (me + s) % n}, device_id_type=MESH)
    pl.semaphore_wait(barrier, n - 1)
    copies = [
        rdma(part.at[(me + s) % n], got.at[s], ps.at[s], pr.at[s], dp=(me + s) % n) for s in range(1, n)
    ]
    for copy in copies:
        copy.start()
    total = part[me]
    for s, copy in enumerate(copies, 1):
        copy.wait_recv()
        total = total + got[s]
    out[me] = finish(total, *[ref[...] for ref in extra])
    backs = [rdma(out.at[me], out.at[me], qs.at[s], qr.at[s], dp=(me + s) % n) for s in range(1, n)]
    for back in backs:
        back.start()
    for s in range(1, n):
        copies[s - 1].wait_send()
        backs[s - 1].wait_send()
        piece = out.at[(me + n - s) % n]
        rdma(piece, piece, qs.at[s], qr.at[s], dp=(me + s) % n).wait_recv()


def vmem(count):
    return [pl.BlockSpec(memory_space=pltpu.VMEM)] * count


def params(number):
    return pltpu.CompilerParams(collective_id=number, has_side_effects=True, vmem_limit_bytes=48 * 1024 * 1024)


def dp_sum(number, finish, part, *extra):
    n, rows, feats = part.shape
    return pl.pallas_call(
        functools.partial(dp_sum_kernel, finish, n),
        out_shape=jax.ShapeDtypeStruct(part.shape, BF16),
        in_specs=vmem(1 + len(extra)),
        out_specs=vmem(1)[0],
        scratch_shapes=[pltpu.VMEM(part.shape, F32)] + [pltpu.SemaphoreType.DMA((n,))] * 4,
        compiler_params=params(number),
    )(part, *extra)


def activate(total, bias, mask):
    return (jnp.maximum(total + bias, 0.0) * mask).astype(BF16)


def pass_grad(total, activation):
    return jnp.where(activation.astype(F32) > 0, total, 0.0).astype(BF16)


def on_device(residuals, enc_w, enc_b, dec_w, dec_b, active):
    layers, width, feats = enc_w.shape
    own = residuals.shape[0]
    rows = 4 * own
    half = width // 2
    tokens = active.shape[0]
    feat = lax.axis_index("feat")
    dp = lax.axis_index("dp")
    quarter = (feat // 32) * 2 + feat % 2
    spread = lax.dynamic_update_slice(
        jnp.zeros((layers, rows, width), BF16), residuals.transpose(1, 0, 2), (0, quarter * own, 0)
    )
    sems3 = [pltpu.SemaphoreType.DMA((3,))] * 2
    gathered = pl.pallas_call(
        gather_kernel,
        out_shape=jax.ShapeDtypeStruct((layers, NZ, rows, width), BF16),
        in_specs=vmem(1),
        out_specs=vmem(1)[0],
        scratch_shapes=[pltpu.VMEM((3, rows, half), BF16)] + sems3 + GATHER_SEMS,
        compiler_params=params(0),
    )(spread)
    flat = gathered.reshape(layers, tokens, width)
    partial_value = jnp.dot(flat[0], enc_w[0], preferred_element_type=F32) + jnp.dot(
        flat[1], enc_w[1], preferred_element_type=F32
    )
    n = tokens // 48
    table = active.reshape(2, NZ, 2, own, -1).transpose(1, 0, 2, 3, 4).reshape(tokens, -1)
    table = lax.dynamic_slice_in_dim(table, dp * 48, 48, 0)
    columns = feat * feats + lax.iota(jnp.int32, feats)
    mask = jnp.any(table[:, :, None] == columns[None, None, :], axis=1).astype(F32)
    activation = dp_sum(1, activate, partial_value.reshape(n, 48, feats), enc_b[None], mask)
    act = activation.reshape(tokens, feats)
    share = jnp.stack(
        [jnp.dot(act, dec_w[l], preferred_element_type=F32) for l in range(layers)]
    ).reshape(layers, NZ, rows, width)
    block = (NZ, rows, half)
    sems16 = pltpu.SemaphoreType.DMA((NZ,))
    grads, recon = pl.pallas_call(
        reduce_kernel,
        out_shape=(
            jax.ShapeDtypeStruct((layers, NZ, rows, width), BF16),
            jax.ShapeDtypeStruct((layers, rows, width), BF16),
        ),
        in_specs=vmem(3),
        out_specs=tuple(vmem(2)),
        scratch_shapes=[pltpu.VMEM(block, F32)] * 2
        + [pltpu.VMEM(block, BF16)] * 4
        + [pltpu.SemaphoreType.DMA((2,))] * 2
        + [sems16] * 4
        + sems3
        + GATHER_SEMS,
        compiler_params=params(2),
    )(share, gathered, dec_b[:, None, :])
    recon = lax.dynamic_slice_in_dim(recon, quarter * own, own, 1).transpose(1, 0, 2)
    rg = grads.reshape(layers, tokens, width)
    dec_bias_grad = jnp.sum(rg.astype(F32), axis=1)
    act_part = sum(
        lax.dot_general(rg[l], dec_w[l], (((1,), (1,)), ((), ())), preferred_element_type=F32) for l in range(layers)
    )
    mine = lax.dynamic_index_in_dim(activation, dp, 0, keepdims=False)
    pre_grad = dp_sum(3, pass_grad, act_part.reshape(n, 48, feats), mine).reshape(tokens, feats)
    enc_bias_grad = jnp.sum(pre_grad.astype(F32), axis=0)
    dec_grad = jnp.einsum("tf,ltd->lfd", act, rg, preferred_element_type=F32).astype(BF16)
    enc_grad = jnp.einsum("ltd,tf->ldf", flat, pre_grad, preferred_element_type=F32).astype(BF16)
    return recon, enc_grad, enc_bias_grad, dec_grad, dec_bias_grad


def solution(mesh):
    return jax.shard_map(
        on_device,
        mesh=mesh,
        in_specs=(
            P("feat", None, "dp"),
            P(None, "dp", "feat"),
            P("feat"),
            P(None, "feat", "dp"),
            P(None, "dp"),
            P(),
        ),
        out_specs=(
            P("feat", None, "dp"),
            P(None, "dp", "feat"),
            P("feat"),
            P(None, "feat", "dp"),
            P(None, "dp"),
        ),
        check_vma=False,
    )
```

```python
import functools

import jax
import jax.numpy as jnp
from jax import lax
from jax.experimental import pallas as pl
from jax.experimental.pallas import tpu as pltpu
from jax.sharding import PartitionSpec as P

MESH = pl.DeviceIdType.MESH
NZ = 16
F32 = jnp.float32
BF16 = jnp.bfloat16


def rdma(src, dst, send, recv, **where):
    return pltpu.make_async_remote_copy(
        src_ref=src, dst_ref=dst, send_sem=send, recv_sem=recv, device_id=where, device_id_type=MESH
    )


def place():
    me = lax.axis_index("feat")
    return me // 32, (me // 2) % NZ, me % 2


def feat_of(y, z, c):
    return (y * NZ + z) * 2 + c


def turn(i):
    odd = i % 2
    return (odd * ((i + 1) // 2) + (1 - odd) * (NZ - i // 2)) % NZ


def greet_feat(reach):
    y, z, c = place()
    barrier = pltpu.get_barrier_semaphore()

    def signal(target):
        pl.semaphore_signal(barrier, inc=1, device_id={"feat": target}, device_id_type=MESH)

    def one(i, carry):
        signal(feat_of(y, (z + i) % NZ, c))
        return carry

    far = min(reach, NZ // 2)
    near = min(reach, NZ // 2 - 1)
    lax.fori_loop(1, far + 1, one, 0)
    lax.fori_loop(NZ - near, NZ, one, 0)
    signal(feat_of(1 - y, z, c))
    signal(feat_of(y, z, 1 - c))
    signal(feat_of(1 - y, z, 1 - c))
    pl.semaphore_wait(barrier, far + near + 3)


def gather_feat(out, sems):
    zs, zr, ys, yr, cs, cr, ds, dr = sems
    y, z, c = place()
    half = out.shape[3] // 2

    def chunk(layer, zz, part):
        return out.at[layer, zz, :, pl.ds(pl.multiple_of(part * half, half), half)]

    def z_copy(held, slot, step):
        piece = chunk(y, (z + NZ - held) % NZ, c)
        return rdma(piece, piece, zs.at[slot], zr.at[slot], feat=feat_of(y, (z + NZ + step) % NZ, c))

    def y_copy(s, layer):
        piece = chunk(layer, (z + NZ - s) % NZ, c)
        return rdma(piece, piece, ys.at[s], yr.at[s], feat=feat_of(1 - y, z, c))

    def c_copy(s, part):
        piece = chunk(y, (z + NZ - s) % NZ, part)
        return rdma(piece, piece, cs.at[s], cr.at[s], feat=feat_of(y, z, 1 - c))

    def d_copy(s, part):
        piece = chunk(1 - y, (z + NZ - s) % NZ, part)
        return rdma(piece, piece, ds.at[s], dr.at[s], feat=feat_of(y, z, 1 - c))

    def forward(i, carry):
        s = turn(i)

        @pl.when(i > 0)
        def _():
            z_copy(s, s, 1).wait_recv()

        @pl.when((i > 0) & (i < 12))
        def _():
            step = 4 * (i % 2) - 2
            z_copy(s, s + step, step).start()

        y_copy(s, y).start()
        c_copy(s, c).start()

        @pl.when(i > 0)
        def _():
            before = turn(i - 1)
            y_copy(before, 1 - y).wait_recv()
            d_copy(before, c).start()

        return carry

    def finish(s, carry):
        @pl.when(s > 0)
        def _():
            z_copy(0, s, 1).wait_send()

        y_copy(s, y).wait_send()
        c_copy(s, c).wait_send()
        d_copy(s, c).wait_send()
        c_copy(s, 1 - c).wait_recv()
        d_copy(s, 1 - c).wait_recv()
        return carry

    for step in (1, -1, 2, -2):
        z_copy(0, step % NZ, step).start()
    lax.fori_loop(0, NZ, forward, 0)
    last = turn(NZ - 1)
    y_copy(last, 1 - y).wait_recv()
    d_copy(last, c).start()
    lax.fori_loop(0, NZ, finish, 0)


GATHER_SEMS = [pltpu.SemaphoreType.DMA((NZ,))] * 8


def others(y, z, c):
    return (feat_of(1 - y, z, c), 1 - y, c), (feat_of(y, z, 1 - c), y, 1 - c), (feat_of(1 - y, z, 1 - c), 1 - y, 1 - c)


def gather_kernel(x_ref, out, got, gs, gr, *sems):
    y, z, c = place()
    half = x_ref.shape[2] // 2

    def cols(part):
        return pl.ds(pl.multiple_of(part * half, half), half)

    greet_feat(2)
    copies = [
        rdma(x_ref.at[yy, :, cols(cc)], got.at[k], gs.at[k], gr.at[k], feat=peer)
        for k, (peer, yy, cc) in enumerate(others(y, z, c))
    ]
    for copy in copies:
        copy.start()
    total = x_ref[y, :, cols(c)].astype(F32)
    for k, copy in enumerate(copies):
        copy.wait_recv()
        total = total + got[k].astype(F32)
    out[y, z, :, cols(c)] = total.astype(BF16)
    gather_feat(out, sems)
    for copy in copies:
        copy.wait_send()


def reduce_kernel(part, resid, bias, grad, recon, ra, rb, ry, rz, sy, sz, ss, sr, ws, wr, vs, vr, gs, gr, *sems):
    y, z, c = place()
    half = part.shape[3] // 2

    def cols(p):
        return pl.ds(pl.multiple_of(p * half, half), half)

    greet_feat(NZ)
    sibling = feat_of(y, z, 1 - c)

    def first(zz):
        return rdma(part.at[1 - y, zz, :, cols(1 - c)], ra.at[zz], ss.at[0, zz], sr.at[0, zz], feat=sibling)

    def second(zz):
        return rdma(part.at[y, zz, :, cols(1 - c)], rb.at[zz], ss.at[1, zz], sr.at[1, zz], feat=sibling)

    def to_c(i, carry):
        zz = (z + turn(NZ - 1 - i)) % NZ
        first(zz).start()
        second(zz).start()
        return carry

    def y_copy(zz):
        return rdma(sy.at[zz], ry.at[zz], ws.at[zz], wr.at[zz], feat=feat_of(1 - y, z, c))

    def z_copy(s):
        return rdma(sz.at[s], rz.at[s], vs.at[s], vr.at[s], feat=feat_of(y, (z + s) % NZ, c))

    def to_y(i, carry):
        zz = (z + turn(NZ - 1 - i)) % NZ
        first(zz).wait_recv()
        sy[zz] = (part[1 - y, zz, :, cols(c)] + ra[zz]).astype(BF16)
        y_copy(zz).start()

        @pl.when(i > 1)
        def _():
            to_z(i - 2)

        return carry

    def to_z(i):
        s = turn(NZ - 1 - i)
        zz = (z + s) % NZ
        y_copy(zz).wait_recv()
        second(zz).wait_recv()
        sz[s] = (part[y, zz, :, cols(c)] + rb[zz] + ry[zz].astype(F32)).astype(BF16)
        z_copy(s).start()

    lax.fori_loop(0, NZ, to_c, 0)
    lax.fori_loop(0, NZ, to_y, 0)
    to_z(NZ - 2)
    y_copy(z).wait_recv()
    second(z).wait_recv()
    total = part[y, z, :, cols(c)] + rb[z] + ry[z].astype(F32)

    def add(i, total):
        s = turn(i)
        z_copy(s).wait_recv()
        return total + rz[s].astype(F32)

    total = lax.fori_loop(1, NZ, add, total)
    full = total + bias[y, :, cols(c)]
    grad[y, z, :, cols(c)] = ((full - resid[y, z, :, cols(c)].astype(F32)) * 0.25).astype(BF16)
    recon[y, :, cols(c)] = full.astype(BF16)
    mine = recon.at[y, :, cols(c)]
    copies = [rdma(mine, mine, gs.at[k], gr.at[k], feat=peer) for k, (peer, _, _) in enumerate(others(y, z, c))]
    for copy in copies:
        copy.start()
    gather_feat(grad, sems)

    def drain(i, carry):
        first(i).wait_send()
        second(i).wait_send()
        y_copy(i).wait_send()

        @pl.when(i > 0)
        def _():
            z_copy(i).wait_send()

        return carry

    lax.fori_loop(0, NZ, drain, 0)
    for k, (peer, yy, cc) in enumerate(others(y, z, c)):
        copies[k].wait_send()
        piece = recon.at[yy, :, cols(cc)]
        rdma(piece, piece, gs.at[k], gr.at[k], feat=peer).wait_recv()


def dp_sum_kernel(finish, n, part, *refs):
    extra, (out, got, ps, pr, qs, qr) = refs[:-6], refs[-6:]
    me = lax.axis_index("dp")
    barrier = pltpu.get_barrier_semaphore()
    for s in range(1, n):
        pl.semaphore_signal(barrier, inc=1, device_id={"dp": (me + s) % n}, device_id_type=MESH)
    pl.semaphore_wait(barrier, n - 1)
    copies = [
        rdma(part.at[(me + s) % n], got.at[s], ps.at[s], pr.at[s], dp=(me + s) % n) for s in range(1, n)
    ]
    for copy in copies:
        copy.start()
    total = part[me]
    for s, copy in enumerate(copies, 1):
        copy.wait_recv()
        total = total + got[s]
    out[me] = finish(total, *[ref[...] for ref in extra])
    backs = [rdma(out.at[me], out.at[me], qs.at[s], qr.at[s], dp=(me + s) % n) for s in range(1, n)]
    for back in backs:
        back.start()
    for s in range(1, n):
        copies[s - 1].wait_send()
        backs[s - 1].wait_send()
        piece = out.at[(me + n - s) % n]
        rdma(piece, piece, qs.at[s], qr.at[s], dp=(me + s) % n).wait_recv()


def vmem(count):
    return [pl.BlockSpec(memory_space=pltpu.VMEM)] * count


def params(number):
    return pltpu.CompilerParams(collective_id=number, has_side_effects=True, vmem_limit_bytes=48 * 1024 * 1024)


def dp_sum(number, finish, part, *extra):
    n, rows, feats = part.shape
    return pl.pallas_call(
        functools.partial(dp_sum_kernel, finish, n),
        out_shape=jax.ShapeDtypeStruct(part.shape, BF16),
        in_specs=vmem(1 + len(extra)),
        out_specs=vmem(1)[0],
        scratch_shapes=[pltpu.VMEM(part.shape, F32)] + [pltpu.SemaphoreType.DMA((n,))] * 4,
        compiler_params=params(number),
    )(part, *extra)


def activate(total, bias, mask):
    return (jnp.maximum(total + bias, 0.0) * mask).astype(BF16)


def pass_grad(total, activation):
    return jnp.where(activation.astype(F32) > 0, total, 0.0).astype(BF16)


def on_device(residuals, enc_w, enc_b, dec_w, dec_b, active):
    layers, width, feats = enc_w.shape
    own = residuals.shape[0]
    rows = 4 * own
    half = width // 2
    tokens = active.shape[0]
    feat = lax.axis_index("feat")
    dp = lax.axis_index("dp")
    quarter = (feat // 32) * 2 + feat % 2
    spread = lax.dynamic_update_slice(
        jnp.zeros((layers, rows, width), BF16), residuals.transpose(1, 0, 2), (0, quarter * own, 0)
    )
    sems3 = [pltpu.SemaphoreType.DMA((3,))] * 2
    gathered = pl.pallas_call(
        gather_kernel,
        out_shape=jax.ShapeDtypeStruct((layers, NZ, rows, width), BF16),
        in_specs=vmem(1),
        out_specs=vmem(1)[0],
        scratch_shapes=[pltpu.VMEM((3, rows, half), BF16)] + sems3 + GATHER_SEMS,
        compiler_params=params(0),
    )(spread)
    flat = gathered.reshape(layers, tokens, width)
    partial_value = jnp.dot(flat[0], enc_w[0], preferred_element_type=F32) + jnp.dot(
        flat[1], enc_w[1], preferred_element_type=F32
    )
    n = tokens // 48
    table = active.reshape(2, NZ, 2, own, -1).transpose(1, 0, 2, 3, 4).reshape(tokens, -1)
    table = lax.dynamic_slice_in_dim(table, dp * 48, 48, 0)
    columns = feat * feats + lax.iota(jnp.int32, feats)
    mask = jnp.any(table[:, :, None] == columns[None, None, :], axis=1).astype(F32)
    activation = dp_sum(1, activate, partial_value.reshape(n, 48, feats), enc_b[None], mask)
    act = activation.reshape(tokens, feats)
    share = jnp.stack(
        [jnp.dot(act, dec_w[l], preferred_element_type=F32) for l in range(layers)]
    ).reshape(layers, NZ, rows, width)
    block = (NZ, rows, half)
    sems16 = pltpu.SemaphoreType.DMA((NZ,))
    grads, recon = pl.pallas_call(
        reduce_kernel,
        out_shape=(
            jax.ShapeDtypeStruct((layers, NZ, rows, width), BF16),
            jax.ShapeDtypeStruct((layers, rows, width), BF16),
        ),
        in_specs=vmem(3),
        out_specs=tuple(vmem(2)),
        scratch_shapes=[pltpu.VMEM(block, F32)] * 2
        + [pltpu.VMEM(block, BF16)] * 4
        + [pltpu.SemaphoreType.DMA((2, NZ))] * 2
        + [sems16] * 4
        + sems3
        + GATHER_SEMS,
        compiler_params=params(2),
    )(share, gathered, dec_b[:, None, :])
    recon = lax.dynamic_slice_in_dim(recon, quarter * own, own, 1).transpose(1, 0, 2)
    rg = grads.reshape(layers, tokens, width)
    dec_bias_grad = jnp.sum(rg.astype(F32), axis=1)
    act_part = sum(
        lax.dot_general(rg[l], dec_w[l], (((1,), (1,)), ((), ())), preferred_element_type=F32) for l in range(layers)
    )
    mine = lax.dynamic_index_in_dim(activation, dp, 0, keepdims=False)
    pre_grad = dp_sum(3, pass_grad, act_part.reshape(n, 48, feats), mine).reshape(tokens, feats)
    enc_bias_grad = jnp.sum(pre_grad.astype(F32), axis=0)
    dec_grad = jnp.einsum("tf,ltd->lfd", act, rg, preferred_element_type=F32).astype(BF16)
    enc_grad = jnp.einsum("ltd,tf->ldf", flat, pre_grad, preferred_element_type=F32).astype(BF16)
    return recon, enc_grad, enc_bias_grad, dec_grad, dec_bias_grad


def solution(mesh):
    return jax.shard_map(
        on_device,
        mesh=mesh,
        in_specs=(
            P("feat", None, "dp"),
            P(None, "dp", "feat"),
            P("feat"),
            P(None, "feat", "dp"),
            P(None, "dp"),
            P(),
        ),
        out_specs=(
            P("feat", None, "dp"),
            P(None, "dp", "feat"),
            P("feat"),
            P(None, "feat", "dp"),
            P(None, "dp"),
        ),
        check_vma=False,
    )
```

```python
import functools

import jax
import jax.numpy as jnp
from jax import lax
from jax.experimental import pallas as pl
from jax.experimental.pallas import tpu as pltpu
from jax.sharding import PartitionSpec as P

MESH = pl.DeviceIdType.MESH
NZ = 16
F32 = jnp.float32
BF16 = jnp.bfloat16


def rdma(src, dst, send, recv, **where):
    return pltpu.make_async_remote_copy(
        src_ref=src, dst_ref=dst, send_sem=send, recv_sem=recv, device_id=where, device_id_type=MESH
    )


def place():
    me = lax.axis_index("feat")
    return me // 32, (me // 2) % NZ, me % 2


def feat_of(y, z, c):
    return (y * NZ + z) * 2 + c


def turn(i):
    odd = i % 2
    return (odd * ((i + 1) // 2) + (1 - odd) * (NZ - i // 2)) % NZ


def greet_feat(reach):
    y, z, c = place()
    barrier = pltpu.get_barrier_semaphore()

    def signal(target):
        pl.semaphore_signal(barrier, inc=1, device_id={"feat": target}, device_id_type=MESH)

    def one(i, carry):
        signal(feat_of(y, (z + i) % NZ, c))
        return carry

    far = min(reach, NZ // 2)
    near = min(reach, NZ // 2 - 1)
    lax.fori_loop(1, far + 1, one, 0)
    lax.fori_loop(NZ - near, NZ, one, 0)
    signal(feat_of(1 - y, z, c))
    signal(feat_of(y, z, 1 - c))
    signal(feat_of(1 - y, z, 1 - c))
    return far + near + 3


def await_greetings(count):
    pl.semaphore_wait(pltpu.get_barrier_semaphore(), count)


def gather_feat(out, sems):
    zs, zr, ys, yr, cs, cr, ds, dr = sems
    y, z, c = place()
    half = out.shape[3] // 2

    def chunk(layer, zz, part):
        return out.at[layer, zz, :, pl.ds(pl.multiple_of(part * half, half), half)]

    def z_copy(held, slot, step):
        piece = chunk(y, (z + NZ - held) % NZ, c)
        return rdma(piece, piece, zs.at[slot], zr.at[slot], feat=feat_of(y, (z + NZ + step) % NZ, c))

    def y_copy(s, layer):
        piece = chunk(layer, (z + NZ - s) % NZ, c)
        return rdma(piece, piece, ys.at[s], yr.at[s], feat=feat_of(1 - y, z, c))

    def c_copy(s, part):
        piece = chunk(y, (z + NZ - s) % NZ, part)
        return rdma(piece, piece, cs.at[s], cr.at[s], feat=feat_of(y, z, 1 - c))

    def d_copy(s, part):
        piece = chunk(1 - y, (z + NZ - s) % NZ, part)
        return rdma(piece, piece, ds.at[s], dr.at[s], feat=feat_of(y, z, 1 - c))

    def forward(i, carry):
        s = turn(i)

        @pl.when(i > 0)
        def _():
            z_copy(s, s, 1).wait_recv()

        @pl.when((i > 0) & (i < 12))
        def _():
            step = 4 * (i % 2) - 2
            z_copy(s, s + step, step).start()

        y_copy(s, y).start()
        c_copy(s, c).start()

        @pl.when(i > 0)
        def _():
            before = turn(i - 1)
            y_copy(before, 1 - y).wait_recv()
            d_copy(before, c).start()

        return carry

    def finish(s, carry):
        @pl.when(s > 0)
        def _():
            z_copy(0, s, 1).wait_send()

        y_copy(s, y).wait_send()
        c_copy(s, c).wait_send()
        d_copy(s, c).wait_send()
        c_copy(s, 1 - c).wait_recv()
        d_copy(s, 1 - c).wait_recv()
        return carry

    for step in (1, -1, 2, -2):
        z_copy(0, step % NZ, step).start()
    lax.fori_loop(0, NZ, forward, 0)
    last = turn(NZ - 1)
    y_copy(last, 1 - y).wait_recv()
    d_copy(last, c).start()
    lax.fori_loop(0, NZ, finish, 0)


GATHER_SEMS = [pltpu.SemaphoreType.DMA((NZ,))] * 8


def others(y, z, c):
    return (feat_of(1 - y, z, c), 1 - y, c), (feat_of(y, z, 1 - c), y, 1 - c), (feat_of(1 - y, z, 1 - c), 1 - y, 1 - c)


def gather_kernel(x_ref, out, got, gs, gr, *sems):
    y, z, c = place()
    half = x_ref.shape[2] // 2

    def cols(part):
        return pl.ds(pl.multiple_of(part * half, half), half)

    await_greetings(greet_feat(2))
    copies = [
        rdma(x_ref.at[yy, :, cols(cc)], got.at[k], gs.at[k], gr.at[k], feat=peer)
        for k, (peer, yy, cc) in enumerate(others(y, z, c))
    ]
    for copy in copies:
        copy.start()
    total = x_ref[y, :, cols(c)].astype(F32)
    for k, copy in enumerate(copies):
        copy.wait_recv()
        total = total + got[k].astype(F32)
    out[y, z, :, cols(c)] = total.astype(BF16)
    gather_feat(out, sems)
    for copy in copies:
        copy.wait_send()


def reduce_kernel(act, dec, resid, bias, grad, recon, part, ra, rb, ry, rz, sy, sz, ss, sr, ws, wr, vs, vr, gs, gr, *sems):
    y, z, c = place()
    half = part.shape[3] // 2

    def cols(p):
        return pl.ds(pl.multiple_of(p * half, half), half)

    count = greet_feat(NZ)
    for layer, p in ((1 - y, 1 - c), (y, 1 - c), (1 - y, c), (y, c)):
        product = jnp.dot(act[...], dec[layer, :, cols(p)], preferred_element_type=F32)
        part[layer, :, :, cols(p)] = product.reshape(NZ, part.shape[2], half)
    await_greetings(count)
    sibling = feat_of(y, z, 1 - c)

    def first(zz):
        return rdma(part.at[1 - y, zz, :, cols(1 - c)], ra.at[zz], ss.at[0, zz], sr.at[0, zz], feat=sibling)

    def second(zz):
        return rdma(part.at[y, zz, :, cols(1 - c)], rb.at[zz], ss.at[1, zz], sr.at[1, zz], feat=sibling)

    def to_c(i, carry):
        zz = (z + turn(NZ - 1 - i)) % NZ
        first(zz).start()
        second(zz).start()
        return carry

    def y_copy(zz):
        return rdma(sy.at[zz], ry.at[zz], ws.at[zz], wr.at[zz], feat=feat_of(1 - y, z, c))

    def z_copy(s):
        return rdma(sz.at[s], rz.at[s], vs.at[s], vr.at[s], feat=feat_of(y, (z + s) % NZ, c))

    def to_y(i, carry):
        zz = (z + turn(NZ - 1 - i)) % NZ
        first(zz).wait_recv()
        sy[zz] = (part[1 - y, zz, :, cols(c)] + ra[zz]).astype(BF16)
        y_copy(zz).start()

        @pl.when(i > 1)
        def _():
            to_z(i - 2)

        return carry

    def to_z(i):
        s = turn(NZ - 1 - i)
        zz = (z + s) % NZ
        y_copy(zz).wait_recv()
        second(zz).wait_recv()
        sz[s] = (part[y, zz, :, cols(c)] + rb[zz] + ry[zz].astype(F32)).astype(BF16)
        z_copy(s).start()

    lax.fori_loop(0, NZ, to_c, 0)
    lax.fori_loop(0, NZ, to_y, 0)
    to_z(NZ - 2)
    y_copy(z).wait_recv()
    second(z).wait_recv()
    total = part[y, z, :, cols(c)] + rb[z] + ry[z].astype(F32)

    def add(i, total):
        s = turn(i)
        z_copy(s).wait_recv()
        return total + rz[s].astype(F32)

    total = lax.fori_loop(1, NZ, add, total)
    full = total + bias[y, :, cols(c)]
    grad[y, z, :, cols(c)] = ((full - resid[y, z, :, cols(c)].astype(F32)) * 0.25).astype(BF16)
    recon[y, :, cols(c)] = full.astype(BF16)
    mine = recon.at[y, :, cols(c)]
    copies = [rdma(mine, mine, gs.at[k], gr.at[k], feat=peer) for k, (peer, _, _) in enumerate(others(y, z, c))]
    for copy in copies:
        copy.start()
    gather_feat(grad, sems)

    def drain(i, carry):
        first(i).wait_send()
        second(i).wait_send()
        y_copy(i).wait_send()

        @pl.when(i > 0)
        def _():
            z_copy(i).wait_send()

        return carry

    lax.fori_loop(0, NZ, drain, 0)
    for k, (peer, yy, cc) in enumerate(others(y, z, c)):
        copies[k].wait_send()
        piece = recon.at[yy, :, cols(cc)]
        rdma(piece, piece, gs.at[k], gr.at[k], feat=peer).wait_recv()


def greet_dp(n):
    me = lax.axis_index("dp")
    barrier = pltpu.get_barrier_semaphore()
    for s in range(1, n):
        pl.semaphore_signal(barrier, inc=1, device_id={"dp": (me + s) % n}, device_id_type=MESH)


def dp_sum(n, part, out, got, ps, pr, qs, qr, finish, meanwhile=None):
    me = lax.axis_index("dp")
    copies = [
        rdma(part.at[(me + s) % n], got.at[s], ps.at[s], pr.at[s], dp=(me + s) % n) for s in range(1, n)
    ]
    for copy in copies:
        copy.start()
    if meanwhile is not None:
        meanwhile()
    total = part[me]
    for s, copy in enumerate(copies, 1):
        copy.wait_recv()
        total = total + got[s]
    out[me] = finish(total, me)
    backs = [rdma(out.at[me], out.at[me], qs.at[s], qr.at[s], dp=(me + s) % n) for s in range(1, n)]
    for back in backs:
        back.start()
    for s in range(1, n):
        copies[s - 1].wait_send()
        backs[s - 1].wait_send()
        piece = out.at[(me + n - s) % n]
        rdma(piece, piece, qs.at[s], qr.at[s], dp=(me + s) % n).wait_recv()


def encode_kernel(n, x, w, bias, mask, out, part, *rest):
    greet_dp(n)
    pre = jnp.dot(x[0], w[0], preferred_element_type=F32)
    for l in range(1, x.shape[0]):
        pre = pre + jnp.dot(x[l], w[l], preferred_element_type=F32)
    part[...] = pre.reshape(part.shape)
    await_greetings(n - 1)

    def activate(total, me):
        return (jnp.maximum(total + bias[...], 0.0) * mask[...]).astype(BF16)

    dp_sum(n, part, out, *rest, activate)


def backward_kernel(n, grad, dec, act, out, dec_grad, part, *rest):
    greet_dp(n)
    contract_last = (((1,), (1,)), ((), ()))
    back = lax.dot_general(grad[0], dec[0], contract_last, preferred_element_type=F32)
    for l in range(1, grad.shape[0]):
        back = back + lax.dot_general(grad[l], dec[l], contract_last, preferred_element_type=F32)
    part[...] = back.reshape(part.shape)
    await_greetings(n - 1)

    def decoder_grad():
        for l in range(grad.shape[0]):
            dec_grad[l] = lax.dot_general(
                act[...].reshape(-1, act.shape[2]), grad[l], (((0,), (0,)), ((), ())), preferred_element_type=F32
            ).astype(BF16)

    def pass_grad(total, me):
        return jnp.where(act[me].astype(F32) > 0, total, 0.0).astype(BF16)

    dp_sum(n, part, out, *rest, pass_grad, decoder_grad)


def vmem(count):
    return [pl.BlockSpec(memory_space=pltpu.VMEM)] * count


def params(number):
    return pltpu.CompilerParams(collective_id=number, has_side_effects=True, vmem_limit_bytes=48 * 1024 * 1024)


def dp_scratch(block):
    return [pltpu.VMEM(block, F32)] * 2 + [pltpu.SemaphoreType.DMA((block[0],))] * 4


def on_device(residuals, enc_w, enc_b, dec_w, dec_b, active):
    layers, width, feats = enc_w.shape
    own = residuals.shape[0]
    rows = 4 * own
    half = width // 2
    tokens = active.shape[0]
    feat = lax.axis_index("feat")
    dp = lax.axis_index("dp")
    quarter = (feat // 32) * 2 + feat % 2
    spread = lax.dynamic_update_slice(
        jnp.zeros((layers, rows, width), BF16), residuals.transpose(1, 0, 2), (0, quarter * own, 0)
    )
    sems3 = [pltpu.SemaphoreType.DMA((3,))] * 2
    gathered = pl.pallas_call(
        gather_kernel,
        out_shape=jax.ShapeDtypeStruct((layers, NZ, rows, width), BF16),
        in_specs=vmem(1),
        out_specs=vmem(1)[0],
        scratch_shapes=[pltpu.VMEM((3, rows, half), BF16)] + sems3 + GATHER_SEMS,
        compiler_params=params(0),
    )(spread)
    flat = gathered.reshape(layers, tokens, width)
    n = tokens // 48
    dp_block = (n, 48, feats)
    table = active.reshape(2, NZ, 2, own, -1).transpose(1, 0, 2, 3, 4).reshape(tokens, -1)
    table = lax.dynamic_slice_in_dim(table, dp * 48, 48, 0)
    columns = feat * feats + lax.iota(jnp.int32, feats)
    mask = jnp.any(table[:, :, None] == columns[None, None, :], axis=1).astype(F32)
    activation = pl.pallas_call(
        functools.partial(encode_kernel, n),
        out_shape=jax.ShapeDtypeStruct(dp_block, BF16),
        in_specs=vmem(4),
        out_specs=vmem(1)[0],
        scratch_shapes=dp_scratch(dp_block),
        compiler_params=params(1),
    )(flat, enc_w, enc_b[None], mask)
    block = (NZ, rows, half)
    sems16 = pltpu.SemaphoreType.DMA((NZ,))
    grads, recon = pl.pallas_call(
        reduce_kernel,
        out_shape=(
            jax.ShapeDtypeStruct((layers, NZ, rows, width), BF16),
            jax.ShapeDtypeStruct((layers, rows, width), BF16),
        ),
        in_specs=vmem(4),
        out_specs=tuple(vmem(2)),
        scratch_shapes=[pltpu.VMEM((layers, NZ, rows, width), F32)]
        + [pltpu.VMEM(block, F32)] * 2
        + [pltpu.VMEM(block, BF16)] * 4
        + [pltpu.SemaphoreType.DMA((2, NZ))] * 2
        + [sems16] * 4
        + sems3
        + GATHER_SEMS,
        compiler_params=params(2),
    )(activation.reshape(tokens, feats), dec_w, gathered, dec_b[:, None, :])
    recon = lax.dynamic_slice_in_dim(recon, quarter * own, own, 1).transpose(1, 0, 2)
    rg = grads.reshape(layers, tokens, width)
    dec_bias_grad = jnp.sum(rg.astype(F32), axis=1)
    pre_grad, dec_grad = pl.pallas_call(
        functools.partial(backward_kernel, n),
        out_shape=(jax.ShapeDtypeStruct(dp_block, BF16), jax.ShapeDtypeStruct(dec_w.shape, BF16)),
        in_specs=vmem(3),
        out_specs=tuple(vmem(2)),
        scratch_shapes=dp_scratch(dp_block),
        compiler_params=params(3),
    )(rg, dec_w, activation)
    pre_grad = pre_grad.reshape(tokens, feats)
    enc_bias_grad = jnp.sum(pre_grad.astype(F32), axis=0)
    enc_grad = jnp.einsum("ltd,tf->ldf", flat, pre_grad, preferred_element_type=F32).astype(BF16)
    return recon, enc_grad, enc_bias_grad, dec_grad, dec_bias_grad


def solution(mesh):
    return jax.shard_map(
        on_device,
        mesh=mesh,
        in_specs=(
            P("feat", None, "dp"),
            P(None, "dp", "feat"),
            P("feat"),
            P(None, "feat", "dp"),
            P(None, "dp"),
            P(),
        ),
        out_specs=(
            P("feat", None, "dp"),
            P(None, "dp", "feat"),
            P("feat"),
            P(None, "feat", "dp"),
            P(None, "dp"),
        ),
        check_vma=False,
    )
```

```python
import functools

import jax
import jax.numpy as jnp
from jax import lax
from jax.experimental import pallas as pl
from jax.experimental.pallas import tpu as pltpu
from jax.sharding import PartitionSpec as P

MESH = pl.DeviceIdType.MESH
NZ = 16
LAG = 5
F32 = jnp.float32
BF16 = jnp.bfloat16


def rdma(src, dst, send, recv, **where):
    return pltpu.make_async_remote_copy(
        src_ref=src, dst_ref=dst, send_sem=send, recv_sem=recv, device_id=where, device_id_type=MESH
    )


def place():
    me = lax.axis_index("feat")
    return me // 32, (me // 2) % NZ, me % 2


def feat_of(y, z, c):
    return (y * NZ + z) * 2 + c


def turn(i):
    odd = i % 2
    return (odd * ((i + 1) // 2) + (1 - odd) * (NZ - i // 2)) % NZ


def greet_feat(reach):
    y, z, c = place()
    barrier = pltpu.get_barrier_semaphore()

    def signal(target):
        pl.semaphore_signal(barrier, inc=1, device_id={"feat": target}, device_id_type=MESH)

    def one(i, carry):
        signal(feat_of(y, (z + i) % NZ, c))
        return carry

    far = min(reach, NZ // 2)
    near = min(reach, NZ // 2 - 1)
    lax.fori_loop(1, far + 1, one, 0)
    lax.fori_loop(NZ - near, NZ, one, 0)
    signal(feat_of(1 - y, z, c))
    signal(feat_of(y, z, 1 - c))
    signal(feat_of(1 - y, z, 1 - c))
    return far + near + 3


def await_greetings(count):
    pl.semaphore_wait(pltpu.get_barrier_semaphore(), count)


def gather_feat(out, sems):
    zs, zr, ys, yr, cs, cr, ds, dr = sems
    y, z, c = place()
    half = out.shape[3] // 2

    def chunk(layer, zz, part):
        return out.at[layer, zz, :, pl.ds(pl.multiple_of(part * half, half), half)]

    def z_copy(held, slot, step):
        piece = chunk(y, (z + NZ - held) % NZ, c)
        return rdma(piece, piece, zs.at[slot], zr.at[slot], feat=feat_of(y, (z + NZ + step) % NZ, c))

    def y_copy(s, layer):
        piece = chunk(layer, (z + NZ - s) % NZ, c)
        return rdma(piece, piece, ys.at[s], yr.at[s], feat=feat_of(1 - y, z, c))

    def c_copy(s, part):
        piece = chunk(y, (z + NZ - s) % NZ, part)
        return rdma(piece, piece, cs.at[s], cr.at[s], feat=feat_of(y, z, 1 - c))

    def d_copy(s, part):
        piece = chunk(1 - y, (z + NZ - s) % NZ, part)
        return rdma(piece, piece, ds.at[s], dr.at[s], feat=feat_of(y, z, 1 - c))

    def forward(i, carry):
        s = turn(i)

        @pl.when(i > 0)
        def _():
            z_copy(s, s, 1).wait_recv()

        @pl.when((i > 0) & (i < 12))
        def _():
            step = 4 * (i % 2) - 2
            z_copy(s, s + step, step).start()

        y_copy(s, y).start()
        c_copy(s, c).start()

        @pl.when(i >= LAG)
        def _():
            pass_on(i - LAG, 0)

        return carry

    def pass_on(i, carry):
        s = turn(i)
        y_copy(s, 1 - y).wait_recv()
        d_copy(s, c).start()
        return carry

    def finish(s, carry):
        @pl.when(s > 0)
        def _():
            z_copy(0, s, 1).wait_send()

        y_copy(s, y).wait_send()
        c_copy(s, c).wait_send()
        d_copy(s, c).wait_send()
        c_copy(s, 1 - c).wait_recv()
        d_copy(s, 1 - c).wait_recv()
        return carry

    for step in (1, -1, 2, -2):
        z_copy(0, step % NZ, step).start()
    lax.fori_loop(0, NZ, forward, 0)
    lax.fori_loop(NZ - LAG, NZ, pass_on, 0)
    lax.fori_loop(0, NZ, finish, 0)


GATHER_SEMS = [pltpu.SemaphoreType.DMA((NZ,))] * 8


def others(y, z, c):
    return (feat_of(1 - y, z, c), 1 - y, c), (feat_of(y, z, 1 - c), y, 1 - c), (feat_of(1 - y, z, 1 - c), 1 - y, 1 - c)


def gather_kernel(x_ref, out, got, gs, gr, *sems):
    y, z, c = place()
    half = x_ref.shape[2] // 2

    def cols(part):
        return pl.ds(pl.multiple_of(part * half, half), half)

    await_greetings(greet_feat(2))
    copies = [
        rdma(x_ref.at[yy, :, cols(cc)], got.at[k], gs.at[k], gr.at[k], feat=peer)
        for k, (peer, yy, cc) in enumerate(others(y, z, c))
    ]
    for copy in copies:
        copy.start()
    total = x_ref[y, :, cols(c)].astype(F32)
    for k, copy in enumerate(copies):
        copy.wait_recv()
        total = total + got[k].astype(F32)
    out[y, z, :, cols(c)] = total.astype(BF16)
    gather_feat(out, sems)
    for copy in copies:
        copy.wait_send()


def reduce_kernel(act, dec, resid, bias, grad, recon, part, ra, rb, ry, rz, sy, sz, ss, sr, ws, wr, vs, vr, gs, gr, *sems):
    y, z, c = place()
    half = part.shape[3] // 2

    def cols(p):
        return pl.ds(pl.multiple_of(p * half, half), half)

    count = greet_feat(NZ)
    for layer, p in ((1 - y, 1 - c), (y, 1 - c), (1 - y, c), (y, c)):
        product = jnp.dot(act[...], dec[layer, :, cols(p)], preferred_element_type=F32)
        part[layer, :, :, cols(p)] = product.reshape(NZ, part.shape[2], half)
    await_greetings(count)
    sibling = feat_of(y, z, 1 - c)

    def first(zz):
        return rdma(part.at[1 - y, zz, :, cols(1 - c)], ra.at[zz], ss.at[0, zz], sr.at[0, zz], feat=sibling)

    def second(zz):
        return rdma(part.at[y, zz, :, cols(1 - c)], rb.at[zz], ss.at[1, zz], sr.at[1, zz], feat=sibling)

    def to_c(i, carry):
        zz = (z + turn(NZ - 1 - i)) % NZ
        first(zz).start()
        second(zz).start()
        return carry

    def y_copy(zz):
        return rdma(sy.at[zz], ry.at[zz], ws.at[zz], wr.at[zz], feat=feat_of(1 - y, z, c))

    def z_copy(s):
        return rdma(sz.at[s], rz.at[s], vs.at[s], vr.at[s], feat=feat_of(y, (z + s) % NZ, c))

    def to_y(i, carry):
        zz = (z + turn(NZ - 1 - i)) % NZ
        first(zz).wait_recv()
        sy[zz] = (part[1 - y, zz, :, cols(c)] + ra[zz]).astype(BF16)
        y_copy(zz).start()

        @pl.when(i >= LAG)
        def _():
            to_z(i - LAG, 0)

        return carry

    def to_z(i, carry):
        s = turn(NZ - 1 - i)
        zz = (z + s) % NZ
        y_copy(zz).wait_recv()
        second(zz).wait_recv()
        sz[s] = (part[y, zz, :, cols(c)] + rb[zz] + ry[zz].astype(F32)).astype(BF16)
        z_copy(s).start()
        return carry

    lax.fori_loop(0, NZ, to_c, 0)
    lax.fori_loop(0, NZ, to_y, 0)
    lax.fori_loop(NZ - LAG, NZ - 1, to_z, 0)
    y_copy(z).wait_recv()
    second(z).wait_recv()
    total = part[y, z, :, cols(c)] + rb[z] + ry[z].astype(F32)

    def add(i, total):
        s = turn(i)
        z_copy(s).wait_recv()
        return total + rz[s].astype(F32)

    total = lax.fori_loop(1, NZ, add, total)
    full = total + bias[y, :, cols(c)]
    grad[y, z, :, cols(c)] = ((full - resid[y, z, :, cols(c)].astype(F32)) * 0.25).astype(BF16)
    recon[y, :, cols(c)] = full.astype(BF16)
    mine = recon.at[y, :, cols(c)]
    copies = [rdma(mine, mine, gs.at[k], gr.at[k], feat=peer) for k, (peer, _, _) in enumerate(others(y, z, c))]
    for copy in copies:
        copy.start()
    gather_feat(grad, sems)

    def drain(i, carry):
        first(i).wait_send()
        second(i).wait_send()
        y_copy(i).wait_send()

        @pl.when(i > 0)
        def _():
            z_copy(i).wait_send()

        return carry

    lax.fori_loop(0, NZ, drain, 0)
    for k, (peer, yy, cc) in enumerate(others(y, z, c)):
        copies[k].wait_send()
        piece = recon.at[yy, :, cols(cc)]
        rdma(piece, piece, gs.at[k], gr.at[k], feat=peer).wait_recv()


def greet_dp(n):
    me = lax.axis_index("dp")
    barrier = pltpu.get_barrier_semaphore()
    for s in range(1, n):
        pl.semaphore_signal(barrier, inc=1, device_id={"dp": (me + s) % n}, device_id_type=MESH)


def dp_sum(n, part, out, got, ps, pr, qs, qr, finish, meanwhile=None):
    me = lax.axis_index("dp")
    copies = [
        rdma(part.at[(me + s) % n], got.at[s], ps.at[s], pr.at[s], dp=(me + s) % n) for s in range(1, n)
    ]
    for copy in copies:
        copy.start()
    if meanwhile is not None:
        meanwhile()
    total = part[me]
    for s, copy in enumerate(copies, 1):
        copy.wait_recv()
        total = total + got[s]
    out[me] = finish(total, me)
    backs = [rdma(out.at[me], out.at[me], qs.at[s], qr.at[s], dp=(me + s) % n) for s in range(1, n)]
    for back in backs:
        back.start()
    for s in range(1, n):
        copies[s - 1].wait_send()
        backs[s - 1].wait_send()
        piece = out.at[(me + n - s) % n]
        rdma(piece, piece, qs.at[s], qr.at[s], dp=(me + s) % n).wait_recv()


def encode_kernel(n, x, w, bias, mask, out, part, *rest):
    greet_dp(n)
    pre = jnp.dot(x[0], w[0], preferred_element_type=F32)
    for l in range(1, x.shape[0]):
        pre = pre + jnp.dot(x[l], w[l], preferred_element_type=F32)
    part[...] = pre.reshape(part.shape)
    await_greetings(n - 1)

    def activate(total, me):
        return (jnp.maximum(total + bias[...], 0.0) * mask[...]).astype(BF16)

    dp_sum(n, part, out, *rest, activate)


def backward_kernel(n, grad, dec, act, out, dec_grad, part, *rest):
    greet_dp(n)
    contract_last = (((1,), (1,)), ((), ()))
    back = lax.dot_general(grad[0], dec[0], contract_last, preferred_element_type=F32)
    for l in range(1, grad.shape[0]):
        back = back + lax.dot_general(grad[l], dec[l], contract_last, preferred_element_type=F32)
    part[...] = back.reshape(part.shape)
    await_greetings(n - 1)

    def decoder_grad():
        for l in range(grad.shape[0]):
            dec_grad[l] = lax.dot_general(
                act[...].reshape(-1, act.shape[2]), grad[l], (((0,), (0,)), ((), ())), preferred_element_type=F32
            ).astype(BF16)

    def pass_grad(total, me):
        return jnp.where(act[me].astype(F32) > 0, total, 0.0).astype(BF16)

    dp_sum(n, part, out, *rest, pass_grad, decoder_grad)


def vmem(count):
    return [pl.BlockSpec(memory_space=pltpu.VMEM)] * count


def params(number):
    return pltpu.CompilerParams(collective_id=number, has_side_effects=True, vmem_limit_bytes=48 * 1024 * 1024)


def dp_scratch(block):
    return [pltpu.VMEM(block, F32)] * 2 + [pltpu.SemaphoreType.DMA((block[0],))] * 4


def on_device(residuals, enc_w, enc_b, dec_w, dec_b, active):
    layers, width, feats = enc_w.shape
    own = residuals.shape[0]
    rows = 4 * own
    half = width // 2
    tokens = active.shape[0]
    feat = lax.axis_index("feat")
    dp = lax.axis_index("dp")
    quarter = (feat // 32) * 2 + feat % 2
    spread = lax.dynamic_update_slice(
        jnp.zeros((layers, rows, width), BF16), residuals.transpose(1, 0, 2), (0, quarter * own, 0)
    )
    sems3 = [pltpu.SemaphoreType.DMA((3,))] * 2
    gathered = pl.pallas_call(
        gather_kernel,
        out_shape=jax.ShapeDtypeStruct((layers, NZ, rows, width), BF16),
        in_specs=vmem(1),
        out_specs=vmem(1)[0],
        scratch_shapes=[pltpu.VMEM((3, rows, half), BF16)] + sems3 + GATHER_SEMS,
        compiler_params=params(0),
    )(spread)
    flat = gathered.reshape(layers, tokens, width)
    n = tokens // 48
    dp_block = (n, 48, feats)
    table = active.reshape(2, NZ, 2, own, -1).transpose(1, 0, 2, 3, 4).reshape(tokens, -1)
    table = lax.dynamic_slice_in_dim(table, dp * 48, 48, 0)
    columns = feat * feats + lax.iota(jnp.int32, feats)
    mask = jnp.any(table[:, :, None] == columns[None, None, :], axis=1).astype(F32)
    activation = pl.pallas_call(
        functools.partial(encode_kernel, n),
        out_shape=jax.ShapeDtypeStruct(dp_block, BF16),
        in_specs=vmem(4),
        out_specs=vmem(1)[0],
        scratch_shapes=dp_scratch(dp_block),
        compiler_params=params(1),
    )(flat, enc_w, enc_b[None], mask)
    block = (NZ, rows, half)
    sems16 = pltpu.SemaphoreType.DMA((NZ,))
    grads, recon = pl.pallas_call(
        reduce_kernel,
        out_shape=(
            jax.ShapeDtypeStruct((layers, NZ, rows, width), BF16),
            jax.ShapeDtypeStruct((layers, rows, width), BF16),
        ),
        in_specs=vmem(4),
        out_specs=tuple(vmem(2)),
        scratch_shapes=[pltpu.VMEM((layers, NZ, rows, width), F32)]
        + [pltpu.VMEM(block, F32)] * 2
        + [pltpu.VMEM(block, BF16)] * 4
        + [pltpu.SemaphoreType.DMA((2, NZ))] * 2
        + [sems16] * 4
        + sems3
        + GATHER_SEMS,
        compiler_params=params(2),
    )(activation.reshape(tokens, feats), dec_w, gathered, dec_b[:, None, :])
    recon = lax.dynamic_slice_in_dim(recon, quarter * own, own, 1).transpose(1, 0, 2)
    rg = grads.reshape(layers, tokens, width)
    dec_bias_grad = jnp.sum(rg.astype(F32), axis=1)
    pre_grad, dec_grad = pl.pallas_call(
        functools.partial(backward_kernel, n),
        out_shape=(jax.ShapeDtypeStruct(dp_block, BF16), jax.ShapeDtypeStruct(dec_w.shape, BF16)),
        in_specs=vmem(3),
        out_specs=tuple(vmem(2)),
        scratch_shapes=dp_scratch(dp_block),
        compiler_params=params(3),
    )(rg, dec_w, activation)
    pre_grad = pre_grad.reshape(tokens, feats)
    enc_bias_grad = jnp.sum(pre_grad.astype(F32), axis=0)
    enc_grad = jnp.einsum("ltd,tf->ldf", flat, pre_grad, preferred_element_type=F32).astype(BF16)
    return recon, enc_grad, enc_bias_grad, dec_grad, dec_bias_grad


def solution(mesh):
    return jax.shard_map(
        on_device,
        mesh=mesh,
        in_specs=(
            P("feat", None, "dp"),
            P(None, "dp", "feat"),
            P("feat"),
            P(None, "feat", "dp"),
            P(None, "dp"),
            P(),
        ),
        out_specs=(
            P("feat", None, "dp"),
            P(None, "dp", "feat"),
            P("feat"),
            P(None, "feat", "dp"),
            P(None, "dp"),
        ),
        check_vma=False,
    )
```

```python
import functools

import jax
import jax.numpy as jnp
from jax import lax
from jax.experimental import pallas as pl
from jax.experimental.pallas import tpu as pltpu
from jax.sharding import PartitionSpec as P

MESH = pl.DeviceIdType.MESH
NZ = 16
LAG = 8
F32 = jnp.float32
BF16 = jnp.bfloat16


def rdma(src, dst, send, recv, **where):
    return pltpu.make_async_remote_copy(
        src_ref=src, dst_ref=dst, send_sem=send, recv_sem=recv, device_id=where, device_id_type=MESH
    )


def place():
    me = lax.axis_index("feat")
    return me // 32, (me // 2) % NZ, me % 2


def feat_of(y, z, c):
    return (y * NZ + z) * 2 + c


def turn(i):
    odd = i % 2
    return (odd * ((i + 1) // 2) + (1 - odd) * (NZ - i // 2)) % NZ


def greet_feat(reach):
    y, z, c = place()
    barrier = pltpu.get_barrier_semaphore()

    def signal(target):
        pl.semaphore_signal(barrier, inc=1, device_id={"feat": target}, device_id_type=MESH)

    def one(i, carry):
        signal(feat_of(y, (z + i) % NZ, c))
        return carry

    far = min(reach, NZ // 2)
    near = min(reach, NZ // 2 - 1)
    lax.fori_loop(1, far + 1, one, 0)
    lax.fori_loop(NZ - near, NZ, one, 0)
    signal(feat_of(1 - y, z, c))
    signal(feat_of(y, z, 1 - c))
    signal(feat_of(1 - y, z, 1 - c))
    return far + near + 3


def await_greetings(count):
    pl.semaphore_wait(pltpu.get_barrier_semaphore(), count)


def gather_feat(out, sems):
    zs, zr, ys, yr, cs, cr, ds, dr = sems
    y, z, c = place()
    half = out.shape[3] // 2

    def chunk(layer, zz, part):
        return out.at[layer, zz, :, pl.ds(pl.multiple_of(part * half, half), half)]

    def z_copy(held, slot, step):
        piece = chunk(y, (z + NZ - held) % NZ, c)
        return rdma(piece, piece, zs.at[slot], zr.at[slot], feat=feat_of(y, (z + NZ + step) % NZ, c))

    def y_copy(s, layer):
        piece = chunk(layer, (z + NZ - s) % NZ, c)
        return rdma(piece, piece, ys.at[s], yr.at[s], feat=feat_of(1 - y, z, c))

    def c_copy(s, part):
        piece = chunk(y, (z + NZ - s) % NZ, part)
        return rdma(piece, piece, cs.at[s], cr.at[s], feat=feat_of(y, z, 1 - c))

    def d_copy(s, part):
        piece = chunk(1 - y, (z + NZ - s) % NZ, part)
        return rdma(piece, piece, ds.at[s], dr.at[s], feat=feat_of(y, z, 1 - c))

    def forward(i, carry):
        s = turn(i)

        @pl.when(i > 0)
        def _():
            z_copy(s, s, 1).wait_recv()

        @pl.when((i > 0) & (i < 12))
        def _():
            step = 4 * (i % 2) - 2
            z_copy(s, s + step, step).start()

        y_copy(s, y).start()
        c_copy(s, c).start()

        @pl.when(i >= LAG)
        def _():
            pass_on(i - LAG, 0)

        return carry

    def pass_on(i, carry):
        s = turn(i)
        y_copy(s, 1 - y).wait_recv()
        d_copy(s, c).start()
        return carry

    def finish(s, carry):
        @pl.when(s > 0)
        def _():
            z_copy(0, s, 1).wait_send()

        y_copy(s, y).wait_send()
        c_copy(s, c).wait_send()
        d_copy(s, c).wait_send()
        c_copy(s, 1 - c).wait_recv()
        d_copy(s, 1 - c).wait_recv()
        return carry

    for step in (1, -1, 2, -2):
        z_copy(0, step % NZ, step).start()
    lax.fori_loop(0, NZ, forward, 0)
    lax.fori_loop(NZ - LAG, NZ, pass_on, 0)
    lax.fori_loop(0, NZ, finish, 0)


GATHER_SEMS = [pltpu.SemaphoreType.DMA((NZ,))] * 8


def others(y, z, c):
    return (feat_of(1 - y, z, c), 1 - y, c), (feat_of(y, z, 1 - c), y, 1 - c), (feat_of(1 - y, z, 1 - c), 1 - y, 1 - c)


def gather_kernel(x_ref, out, got, gs, gr, *sems):
    y, z, c = place()
    half = x_ref.shape[2] // 2

    def cols(part):
        return pl.ds(pl.multiple_of(part * half, half), half)

    await_greetings(greet_feat(2))
    copies = [
        rdma(x_ref.at[yy, :, cols(cc)], got.at[k], gs.at[k], gr.at[k], feat=peer)
        for k, (peer, yy, cc) in enumerate(others(y, z, c))
    ]
    for copy in copies:
        copy.start()
    total = x_ref[y, :, cols(c)].astype(F32)
    for k, copy in enumerate(copies):
        copy.wait_recv()
        total = total + got[k].astype(F32)
    out[y, z, :, cols(c)] = total.astype(BF16)
    gather_feat(out, sems)
    for copy in copies:
        copy.wait_send()


def reduce_kernel(act, dec, resid, bias, grad, recon, part, ra, rb, ry, rz, sy, sz, ss, sr, ws, wr, vs, vr, gs, gr, *sems):
    y, z, c = place()
    half = part.shape[3] // 2

    def cols(p):
        return pl.ds(pl.multiple_of(p * half, half), half)

    count = greet_feat(NZ)
    for layer, p in ((1 - y, 1 - c), (y, 1 - c), (1 - y, c), (y, c)):
        product = jnp.dot(act[...], dec[layer, :, cols(p)], preferred_element_type=F32)
        part[layer, :, :, cols(p)] = product.reshape(NZ, part.shape[2], half)
    await_greetings(count)
    sibling = feat_of(y, z, 1 - c)

    def first(zz):
        return rdma(part.at[1 - y, zz, :, cols(1 - c)], ra.at[zz], ss.at[0, zz], sr.at[0, zz], feat=sibling)

    def second(zz):
        return rdma(part.at[y, zz, :, cols(1 - c)], rb.at[zz], ss.at[1, zz], sr.at[1, zz], feat=sibling)

    def to_c(i, carry):
        zz = (z + turn(NZ - 1 - i)) % NZ
        first(zz).start()
        second(zz).start()
        return carry

    def y_copy(zz):
        return rdma(sy.at[zz], ry.at[zz], ws.at[zz], wr.at[zz], feat=feat_of(1 - y, z, c))

    def z_copy(s):
        return rdma(sz.at[s], rz.at[s], vs.at[s], vr.at[s], feat=feat_of(y, (z + s) % NZ, c))

    def to_y(i, carry):
        zz = (z + turn(NZ - 1 - i)) % NZ
        first(zz).wait_recv()
        sy[zz] = (part[1 - y, zz, :, cols(c)] + ra[zz]).astype(BF16)
        y_copy(zz).start()

        @pl.when(i >= LAG)
        def _():
            to_z(i - LAG, 0)

        return carry

    def to_z(i, carry):
        s = turn(NZ - 1 - i)
        zz = (z + s) % NZ
        y_copy(zz).wait_recv()
        second(zz).wait_recv()
        sz[s] = (part[y, zz, :, cols(c)] + rb[zz] + ry[zz].astype(F32)).astype(BF16)
        z_copy(s).start()
        return carry

    lax.fori_loop(0, NZ, to_c, 0)
    lax.fori_loop(0, NZ, to_y, 0)
    lax.fori_loop(NZ - LAG, NZ - 1, to_z, 0)
    y_copy(z).wait_recv()
    second(z).wait_recv()
    total = part[y, z, :, cols(c)] + rb[z] + ry[z].astype(F32)

    def add(i, total):
        s = turn(i)
        z_copy(s).wait_recv()
        return total + rz[s].astype(F32)

    total = lax.fori_loop(1, NZ, add, total)
    full = total + bias[y, :, cols(c)]
    grad[y, z, :, cols(c)] = ((full - resid[y, z, :, cols(c)].astype(F32)) * 0.25).astype(BF16)
    recon[y, :, cols(c)] = full.astype(BF16)
    mine = recon.at[y, :, cols(c)]
    copies = [rdma(mine, mine, gs.at[k], gr.at[k], feat=peer) for k, (peer, _, _) in enumerate(others(y, z, c))]
    for copy in copies:
        copy.start()
    gather_feat(grad, sems)

    def drain(i, carry):
        first(i).wait_send()
        second(i).wait_send()
        y_copy(i).wait_send()

        @pl.when(i > 0)
        def _():
            z_copy(i).wait_send()

        return carry

    lax.fori_loop(0, NZ, drain, 0)
    for k, (peer, yy, cc) in enumerate(others(y, z, c)):
        copies[k].wait_send()
        piece = recon.at[yy, :, cols(cc)]
        rdma(piece, piece, gs.at[k], gr.at[k], feat=peer).wait_recv()


def greet_dp(n):
    me = lax.axis_index("dp")
    barrier = pltpu.get_barrier_semaphore()
    for s in range(1, n):
        pl.semaphore_signal(barrier, inc=1, device_id={"dp": (me + s) % n}, device_id_type=MESH)


def dp_sum(n, part, out, got, ps, pr, qs, qr, finish, meanwhile=None):
    me = lax.axis_index("dp")
    copies = [
        rdma(part.at[(me + s) % n], got.at[s], ps.at[s], pr.at[s], dp=(me + s) % n) for s in range(1, n)
    ]
    for copy in copies:
        copy.start()
    if meanwhile is not None:
        meanwhile()
    total = part[me]
    for s, copy in enumerate(copies, 1):
        copy.wait_recv()
        total = total + got[s]
    out[me] = finish(total, me)
    backs = [rdma(out.at[me], out.at[me], qs.at[s], qr.at[s], dp=(me + s) % n) for s in range(1, n)]
    for back in backs:
        back.start()
    for s in range(1, n):
        copies[s - 1].wait_send()
        backs[s - 1].wait_send()
        piece = out.at[(me + n - s) % n]
        rdma(piece, piece, qs.at[s], qr.at[s], dp=(me + s) % n).wait_recv()


def encode_kernel(n, x, w, bias, mask, out, part, *rest):
    greet_dp(n)
    pre = jnp.dot(x[0], w[0], preferred_element_type=F32)
    for l in range(1, x.shape[0]):
        pre = pre + jnp.dot(x[l], w[l], preferred_element_type=F32)
    part[...] = pre.reshape(part.shape)
    await_greetings(n - 1)

    def activate(total, me):
        return (jnp.maximum(total + bias[...], 0.0) * mask[...]).astype(BF16)

    dp_sum(n, part, out, *rest, activate)


def backward_kernel(n, grad, dec, act, out, dec_grad, part, *rest):
    greet_dp(n)
    contract_last = (((1,), (1,)), ((), ()))
    back = lax.dot_general(grad[0], dec[0], contract_last, preferred_element_type=F32)
    for l in range(1, grad.shape[0]):
        back = back + lax.dot_general(grad[l], dec[l], contract_last, preferred_element_type=F32)
    part[...] = back.reshape(part.shape)
    await_greetings(n - 1)

    def decoder_grad():
        for l in range(grad.shape[0]):
            dec_grad[l] = lax.dot_general(
                act[...].reshape(-1, act.shape[2]), grad[l], (((0,), (0,)), ((), ())), preferred_element_type=F32
            ).astype(BF16)

    def pass_grad(total, me):
        return jnp.where(act[me].astype(F32) > 0, total, 0.0).astype(BF16)

    dp_sum(n, part, out, *rest, pass_grad, decoder_grad)


def vmem(count):
    return [pl.BlockSpec(memory_space=pltpu.VMEM)] * count


def params(number):
    return pltpu.CompilerParams(collective_id=number, has_side_effects=True, vmem_limit_bytes=48 * 1024 * 1024)


def dp_scratch(block):
    return [pltpu.VMEM(block, F32)] * 2 + [pltpu.SemaphoreType.DMA((block[0],))] * 4


def on_device(residuals, enc_w, enc_b, dec_w, dec_b, active):
    layers, width, feats = enc_w.shape
    own = residuals.shape[0]
    rows = 4 * own
    half = width // 2
    tokens = active.shape[0]
    feat = lax.axis_index("feat")
    dp = lax.axis_index("dp")
    quarter = (feat // 32) * 2 + feat % 2
    spread = lax.dynamic_update_slice(
        jnp.zeros((layers, rows, width), BF16), residuals.transpose(1, 0, 2), (0, quarter * own, 0)
    )
    sems3 = [pltpu.SemaphoreType.DMA((3,))] * 2
    gathered = pl.pallas_call(
        gather_kernel,
        out_shape=jax.ShapeDtypeStruct((layers, NZ, rows, width), BF16),
        in_specs=vmem(1),
        out_specs=vmem(1)[0],
        scratch_shapes=[pltpu.VMEM((3, rows, half), BF16)] + sems3 + GATHER_SEMS,
        compiler_params=params(0),
    )(spread)
    flat = gathered.reshape(layers, tokens, width)
    n = tokens // 48
    dp_block = (n, 48, feats)
    table = active.reshape(2, NZ, 2, own, -1).transpose(1, 0, 2, 3, 4).reshape(tokens, -1)
    table = lax.dynamic_slice_in_dim(table, dp * 48, 48, 0)
    columns = feat * feats + lax.iota(jnp.int32, feats)
    mask = jnp.any(table[:, :, None] == columns[None, None, :], axis=1).astype(F32)
    activation = pl.pallas_call(
        functools.partial(encode_kernel, n),
        out_shape=jax.ShapeDtypeStruct(dp_block, BF16),
        in_specs=vmem(4),
        out_specs=vmem(1)[0],
        scratch_shapes=dp_scratch(dp_block),
        compiler_params=params(1),
    )(flat, enc_w, enc_b[None], mask)
    block = (NZ, rows, half)
    sems16 = pltpu.SemaphoreType.DMA((NZ,))
    grads, recon = pl.pallas_call(
        reduce_kernel,
        out_shape=(
            jax.ShapeDtypeStruct((layers, NZ, rows, width), BF16),
            jax.ShapeDtypeStruct((layers, rows, width), BF16),
        ),
        in_specs=vmem(4),
        out_specs=tuple(vmem(2)),
        scratch_shapes=[pltpu.VMEM((layers, NZ, rows, width), F32)]
        + [pltpu.VMEM(block, F32)] * 2
        + [pltpu.VMEM(block, BF16)] * 4
        + [pltpu.SemaphoreType.DMA((2, NZ))] * 2
        + [sems16] * 4
        + sems3
        + GATHER_SEMS,
        compiler_params=params(2),
    )(activation.reshape(tokens, feats), dec_w, gathered, dec_b[:, None, :])
    recon = lax.dynamic_slice_in_dim(recon, quarter * own, own, 1).transpose(1, 0, 2)
    rg = grads.reshape(layers, tokens, width)
    dec_bias_grad = jnp.sum(rg.astype(F32), axis=1)
    pre_grad, dec_grad = pl.pallas_call(
        functools.partial(backward_kernel, n),
        out_shape=(jax.ShapeDtypeStruct(dp_block, BF16), jax.ShapeDtypeStruct(dec_w.shape, BF16)),
        in_specs=vmem(3),
        out_specs=tuple(vmem(2)),
        scratch_shapes=dp_scratch(dp_block),
        compiler_params=params(3),
    )(rg, dec_w, activation)
    pre_grad = pre_grad.reshape(tokens, feats)
    enc_bias_grad = jnp.sum(pre_grad.astype(F32), axis=0)
    enc_grad = jnp.einsum("ltd,tf->ldf", flat, pre_grad, preferred_element_type=F32).astype(BF16)
    return recon, enc_grad, enc_bias_grad, dec_grad, dec_bias_grad


def solution(mesh):
    return jax.shard_map(
        on_device,
        mesh=mesh,
        in_specs=(
            P("feat", None, "dp"),
            P(None, "dp", "feat"),
            P("feat"),
            P(None, "feat", "dp"),
            P(None, "dp"),
            P(),
        ),
        out_specs=(
            P("feat", None, "dp"),
            P(None, "dp", "feat"),
            P("feat"),
            P(None, "feat", "dp"),
            P(None, "dp"),
        ),
        check_vma=False,
    )
```
